1024 devices in a mesh: wall: 64 (over x, z_lo), span: 16 (over y, z_hi, core).
Axes of the slice: x: 4, y: 4, z: 32 (z_hi: 2, z_lo: 16; z = z_hi * 16 + z_lo), core: 2. Of those that a mesh axis runs over, the one named last changes fastest.
Arguments:
- velocity: bfloat16 [2, 8, 1536, 4096], P(None, None, 'wall', 'span')
- kx_index: int32 [8], replicated, may hold values from 0 to 5119
- kz_index: int32 [4096], P('span'), may hold values from 0 to 4095
- helm_even: bfloat16 [768, 768], replicated, may hold values from -0.21875 to 0.21875
- helm_odd: bfloat16 [768, 768], replicated, may hold values from -0.21875 to 0.21875
- deriv_even: bfloat16 [768, 768], replicated, may hold values from -0.21875 to 0.21875
- deriv_odd: bfloat16 [768, 768], replicated, may hold values from -0.21875 to 0.21875
Outputs:
- updated: bfloat16 [2, 8, 1536, 4096], P(None, None, 'wall', 'span')
- shear: bfloat16 [2, 8, 1536, 4096], P(None, None, 'wall', 'span')
The draws below stay inside these ranges and needn't reach their ends.
All inputs are finite; a program needn't handle non-finite values.
Results may differ from the reference program's by a relative error of at most 0.008.
Values may be sent and summed in bfloat16 or wider, within the bound.
A program may use at most 32 MiB of HBM per device.

```python
import jax
import jax.numpy as jnp
from jax import lax

NY = 1536
KZ = 4096
XMODES = 5120
KX = 8


def draw_velocity(key, part):
    key_base, key_plane, key_span = jax.random.split(key, 3)
    plane_ramp = jnp.exp(jnp.log(0.4) + jnp.log(4.0) * jnp.arange(NY, dtype=jnp.float32) / NY)
    plane_ramp = plane_ramp * jnp.exp(jax.random.uniform(key_plane, (NY,), jnp.float32, -0.35, 0.35))
    span_ramp = 0.6 + 0.9 * jnp.arange(KZ, dtype=jnp.float32) / KZ
    span_ramp = span_ramp * jnp.exp(jax.random.uniform(key_span, (KZ,), jnp.float32, -0.35, 0.35))
    base = jax.random.normal(key_base, (2, KX, NY, KZ), jnp.float32)
    return (base * plane_ramp[None, None, :, None] * span_ramp[None, None, None, :]).astype(jnp.bfloat16)


def set_ends(array, rng, smallest, high):
    place = [jax.random.randint(jax.random.fold_in(rng, axis), (), 0, length) for axis, length in enumerate(array.shape)]
    widest = array.shape.index(max(array.shape))
    beside = place[:widest] + [(place[widest] + 1) % array.shape[widest]] + place[widest + 1:]
    return array.at[tuple(place)].set(smallest).at[tuple(beside)].set(high)


def normal_values(own_key, dims, scale, limit, kind=jnp.bfloat16):
    drawn = scale * jax.random.normal(own_key, dims, jnp.float32)
    return jnp.clip(drawn, min=-limit, max=limit).astype(kind)


def setup_inputs(seed: int = 0) -> dict:
    keys = jax.random.split(jax.random.key(seed), 8)
    velocity = draw_velocity(jax.random.fold_in(keys[7], 71), 0)
    kx_index = set_ends(jax.random.randint(keys[1], (KX,), 0, XMODES), jax.random.fold_in(keys[1], 1), 0, XMODES - 1).astype(jnp.int32)
    kz_index = set_ends(jax.random.randint(keys[2], (KZ,), 0, KZ), jax.random.fold_in(keys[2], 1), 0, KZ - 1).astype(jnp.int32)
    helm_even = normal_values(keys[3], (NY // 2, NY // 2), (NY // 2) ** -0.5, 0.21875)
    helm_odd = normal_values(keys[4], (NY // 2, NY // 2), (NY // 2) ** -0.5, 0.21875)
    deriv_even = normal_values(keys[5], (NY // 2, NY // 2), (NY // 2) ** -0.5, 0.21875)
    deriv_odd = normal_values(keys[6], (NY // 2, NY // 2), (NY // 2) ** -0.5, 0.21875)
    return dict(velocity=velocity, kx_index=kx_index, kz_index=kz_index, helm_even=helm_even, helm_odd=helm_odd, deriv_even=deriv_even, deriv_odd=deriv_odd)


def slab_energy(plane):
    wide = plane.astype(jnp.float32)
    return jnp.sum(wide * wide)


def reference(velocity, kx_index, kz_index, helm_even, helm_odd, deriv_even, deriv_odd):
    half = NY // 2
    energy = jnp.sum(lax.map(slab_energy, jnp.moveaxis(velocity, 1, 0)))
    scale = jnp.float32(2.0 * KX * NY * KZ) / energy
    heven_mat = helm_even.astype(jnp.float32)
    hodd_mat = helm_odd.astype(jnp.float32)
    deven_mat = deriv_even.astype(jnp.float32)
    dodd_mat = deriv_odd.astype(jnp.float32)
    kz_sq = (kz_index.astype(jnp.float32) / KZ) ** 2

    def one_slab(inputs):
        plane, wave = inputs
        wide = plane.astype(jnp.float32)
        flip = wide[:, ::-1, :]
        even = ((wide[:, :half] + flip[:, :half]) * 0.5).astype(jnp.bfloat16)
        odd = ((wide[:, :half] - flip[:, :half]) * 0.5).astype(jnp.bfloat16)
        heven = jnp.einsum("cjz,ij->ciz", even.astype(jnp.float32), heven_mat).astype(jnp.bfloat16)
        hodd = jnp.einsum("cjz,ij->ciz", odd.astype(jnp.float32), hodd_mat).astype(jnp.bfloat16)
        he32 = heven.astype(jnp.float32)
        ho32 = hodd.astype(jnp.float32)
        dodd = jnp.einsum("cjz,ij->ciz", he32, deven_mat)
        deven = jnp.einsum("cjz,ij->ciz", ho32, dodd_mat)
        lines_u = jnp.concatenate([he32 + ho32, (he32 - ho32)[:, ::-1]], axis=1).astype(jnp.bfloat16)
        lines_d = jnp.concatenate([deven + dodd, (deven - dodd)[:, ::-1]], axis=1).astype(jnp.bfloat16)
        damp = 1.0 / (1.0 + 2.0 * ((wave.astype(jnp.float32) / XMODES) ** 2 + kz_sq))
        factor = scale * damp
        updated = (factor * lines_u.astype(jnp.float32)).astype(jnp.bfloat16)
        shear = (factor * lines_d.astype(jnp.float32)).astype(jnp.bfloat16)
        return updated, shear

    updated, shear = lax.map(one_slab, (jnp.moveaxis(velocity, 1, 0), kx_index))
    return jnp.moveaxis(updated, 0, 1), jnp.moveaxis(shear, 0, 1)
```

```python
import functools

import jax
import jax.numpy as jnp
from jax import lax
from jax.experimental import pallas as pl
from jax.experimental.pallas import tpu as pltpu
from jax.sharding import PartitionSpec as P

NY = 1536
KZ = 4096
XMODES = 5120
KX = 8
HALF = NY // 2
NX = 4
NZ = 16
NB = 24
NL = 128
NC = 2
OWN = NZ * NB
MESH = pl.DeviceIdType.MESH


def kernel(
    v_hbm, kx_ref, kz_ref, he_hbm, ho_hbm, de_hbm, do_hbm,
    outu_ref, outd_ref,
    v_scr, rx, tx, rxo, he, ho, de, do, e1, e2, e3, e4,
    loc_sem, w_sem, zs, zr, xs, xr, bs, br, es1, er1, es2, er2, es3, er3, es4, er4,
):
    f32, bf16 = jnp.float32, jnp.bfloat16
    wall = lax.axis_index("wall")
    span = lax.axis_index("span")
    x, z = wall // NZ, wall % NZ
    yy, zh, core = span // 4, (span // 2) % 2, span % 2
    yc = yy * 2 + core

    def zdev(d):
        return (x * NZ + (z + d) % NZ, span)

    def xdev(d):
        return (((x + d) % NX) * NZ + z, span)

    def ycdev(d):
        t = (yc + d) % 8
        return (wall, ((t // 2) * 2 + zh) * 2 + t % 2)

    hdev = (wall, (yy * 2 + (1 - zh)) * 2 + core)

    vcopies = []
    for h in range(NC):
        c = pltpu.make_async_copy(v_hbm.at[:, :, pl.ds(h * NL, NL)], v_scr.at[h], loc_sem.at[h])
        c.start()
        vcopies.append(c)
    i0 = ((x + 1) // 2 % 2) * OWN
    i0 = pl.multiple_of(i0, OWN)
    wcopies = [
        pltpu.make_async_copy(he_hbm, he, w_sem.at[0]),
        pltpu.make_async_copy(ho_hbm, ho, w_sem.at[1]),
        pltpu.make_async_copy(de_hbm.at[pl.ds(i0, OWN), :], de, w_sem.at[2]),
        pltpu.make_async_copy(do_hbm.at[pl.ds(i0, OWN), :], do, w_sem.at[3]),
    ]
    for c in wcopies:
        c.start()

    barrier = pltpu.get_barrier_semaphore()

    def greet(dev):
        pl.semaphore_signal(barrier, inc=1, device_id=dev, device_id_type=MESH)

    greet(hdev)

    def greet_z(d, carry):
        greet(zdev(d))
        return carry

    lax.fori_loop(1, NZ, greet_z, 0)
    for d in range(1, NX):
        greet(xdev(d))
    for d in range(1, 8):
        greet(ycdev(d))

    for c in vcopies:
        c.wait()
    part = jnp.zeros((8, NL), f32)
    for h in range(NC):
        for c in range(NZ):
            w = v_scr[h, c].astype(f32)
            w = w * w
            part = part + (w[0:8] + w[8:16] + w[16:24])
    e1[yc] = jnp.sum(part, axis=0, keepdims=True)

    pl.semaphore_wait(barrier, 1 + (NZ - 1) + (NX - 1) + 7)

    def zcopy(h, d):
        p = (z + d) % NZ
        return pltpu.make_async_remote_copy(
            src_ref=v_scr.at[h, p], dst_ref=rx.at[h, x * NZ + z],
            send_sem=zs.at[h, d], recv_sem=zr.at[h, z],
            device_id=(x * NZ + p, span), device_id_type=MESH,
        )

    def zwait(h, q):
        pltpu.make_async_remote_copy(
            src_ref=v_scr.at[h, q], dst_ref=rx.at[h, x * NZ + q],
            send_sem=zs.at[h, 0], recv_sem=zr.at[h, q],
            device_id=hdev, device_id_type=MESH,
        ).wait_recv()

    for h in range(NC):
        zcopy(h, 8).start()

        def send_z(m, carry, h=h):
            zcopy(h, 8 - m).start()
            zcopy(h, 8 + m).start()
            return carry

        lax.fori_loop(1, 8, send_z, 0)
        pltpu.make_async_copy(v_scr.at[h, z], rx.at[h, x * NZ + z], zr.at[h, z]).start()

    def ecopy(buf, slot, d, ss, rs, dev):
        return pltpu.make_async_remote_copy(
            src_ref=buf.at[slot], dst_ref=buf.at[slot], send_sem=ss.at[d], recv_sem=rs.at[slot],
            device_id=dev, device_id_type=MESH,
        )

    for d in range(1, 8):
        ecopy(e1, yc, d, es1, er1, ycdev(d)).start()

    rows = lax.broadcasted_iota(jnp.int32, (256, 256), 0)
    cols = lax.broadcasted_iota(jnp.int32, (256, 256), 1)
    flip256 = jnp.where(rows + cols == 255, 1.0, 0.0).astype(bf16)
    flip128 = flip256[0:128, 128:256]
    mirrored = x >= 2
    sign = jnp.where(mirrored, -1.0, 1.0).astype(f32)

    def xcopy(h, d):
        blocks = pl.ds(x * NZ, NZ)
        return pltpu.make_async_remote_copy(
            src_ref=rx.at[h, blocks], dst_ref=rx.at[h, blocks],
            send_sem=xs.at[h, d], recv_sem=xr.at[h, d],
            device_id=xdev(d), device_id_type=MESH,
        )

    def xwait(h, d):
        src = ((x + NX - d) % NX) * NZ
        pltpu.make_async_remote_copy(
            src_ref=rx.at[h, pl.ds(src, NZ)], dst_ref=rx.at[h, pl.ds(src, NZ)],
            send_sem=xs.at[h, d], recv_sem=xr.at[h, d],
            device_id=xdev(d), device_id_type=MESH,
        ).wait_recv()

    def bcopy(h, t, d):
        p = (z + d) % NZ
        return pltpu.make_async_remote_copy(
            src_ref=tx.at[h, t, p], dst_ref=rxo.at[h, t, z],
            send_sem=bs.at[h, t, d], recv_sem=br.at[h, t, z],
            device_id=(x * NZ + p, span), device_id_type=MESH,
        )

    def compute(h):
        lo = rx[h, 0:32].astype(f32).reshape(HALF, NL)
        hi = rx[h, 32:64].astype(f32).reshape(HALF, NL).astype(bf16)
        fl = jnp.concatenate(
            [jnp.dot(flip256, hi[HALF - 256 * (b + 1):HALF - 256 * b], preferred_element_type=f32) for b in range(3)],
            axis=0,
        )
        even = ((lo + fl) * 0.5).astype(bf16)
        odd = ((lo - fl) * 0.5).astype(bf16)
        heven = jnp.dot(he[...], even, preferred_element_type=f32).astype(bf16)
        hodd = jnp.dot(ho[...], odd, preferred_element_type=f32).astype(bf16)
        dodd = jnp.dot(de[...], heven, preferred_element_type=f32)
        deven = jnp.dot(do[...], hodd, preferred_element_type=f32)
        he32, ho32 = heven.astype(f32), hodd.astype(f32)
        upper = i0 > 0
        hes = jnp.where(upper, he32[OWN:], he32[:OWN])
        hos = jnp.where(upper, ho32[OWN:], ho32[:OWN])

        def place(t, lines):
            back = jnp.concatenate(
                [jnp.dot(flip128, lines[OWN - 128 * (b + 1):OWN - 128 * b], preferred_element_type=f32) for b in range(3)],
                axis=0,
            )
            res = jnp.where(mirrored, back, lines.astype(f32))
            tx[h, t] = res.reshape(NZ, NB, NL).astype(bf16)

        place(0, (hes + sign * hos).astype(bf16))
        place(1, (deven + sign * dodd).astype(bf16))

    for h in range(NC):
        lax.fori_loop(0, NZ, lambda q, c, h=h: (zwait(h, q), c)[1], 0)
        for d in range(1, NX):
            xcopy(h, d).start()
        if h == 0:
            for c in wcopies:
                c.wait()
            for d in range(1, 8):
                ecopy(e1, (yc + d) % 8, d, es1, er1, hdev).wait_recv()
            e2[x] = jnp.sum(e1[...], axis=0)
            for d in range(1, NX):
                ecopy(e2, x, d, es2, er2, xdev(d)).start()
        for d in range(1, NX):
            xwait(h, d)
        compute(h)
        for t in range(2):
            bcopy(h, t, 8).start()

            def send_b(m, carry, h=h, t=t):
                bcopy(h, t, 8 - m).start()
                bcopy(h, t, 8 + m).start()
                return carry

            lax.fori_loop(1, 8, send_b, 0)
            pltpu.make_async_copy(tx.at[h, t, z], rxo.at[h, t, z], br.at[h, t, z]).start()
        if h == 0:
            for d in range(1, NX):
                ecopy(e2, (x + d) % NX, d, es2, er2, hdev).wait_recv()
            e3[zh] = jnp.sum(e2[...], axis=0)
            ecopy(e3, zh, 0, es3, er3, hdev).start()
        else:
            ecopy(e3, 1 - zh, 0, es3, er3, hdev).wait_recv()
            e4[z] = jnp.sum(e3[...], axis=0)

            def send_e4(d, carry):
                ecopy(e4, z, d, es4, er4, zdev(d)).start()
                return carry

            lax.fori_loop(1, NZ, send_e4, 0)

    kz = kz_ref[...].astype(f32) / KZ
    kz_sq = kz * kz

    def wait_e4(d, carry):
        ecopy(e4, (z + d) % NZ, d, es4, er4, hdev).wait_recv()
        return carry

    lax.fori_loop(1, NZ, wait_e4, 0)
    energy = jnp.sum(jnp.sum(e4[...], axis=0), axis=1, keepdims=True)
    scale = jnp.float32(2.0 * KX * NY * KZ) / energy
    factors = []
    for k in range(KX):
        kx = kx_ref[k].astype(f32) / XMODES
        factors.append(scale * (1.0 / (1.0 + 2.0 * (kx * kx + kz_sq))))

    def bwait(h, t, c):
        pltpu.make_async_remote_copy(
            src_ref=tx.at[h, t, c], dst_ref=rxo.at[h, t, c],
            send_sem=bs.at[h, t, 0], recv_sem=br.at[h, t, c],
            device_id=hdev, device_id_type=MESH,
        ).wait_recv()

    for h in range(NC):
        for t, out in enumerate((outu_ref, outd_ref)):
            lax.fori_loop(0, NZ, lambda c, carry, h=h, t=t: (bwait(h, t, c), carry)[1], 0)
            for c in range(NZ):
                f = factors[c % KX][:, h * NL:(h + 1) * NL]
                out[c, :, h * NL:(h + 1) * NL] = (f * rxo[h, t, c].astype(f32)).astype(bf16)

    def drain(d, carry):
        for h in range(NC):
            zcopy(h, d).wait_send()
            for t in range(2):
                bcopy(h, t, d).wait_send()
        ecopy(e4, z, d, es4, er4, zdev(d)).wait_send()
        return carry

    lax.fori_loop(1, NZ, drain, 0)
    for d in range(1, NX):
        for h in range(NC):
            xcopy(h, d).wait_send()
        ecopy(e2, x, d, es2, er2, xdev(d)).wait_send()
    for d in range(1, 8):
        ecopy(e1, yc, d, es1, er1, ycdev(d)).wait_send()
    ecopy(e3, zh, 0, es3, er3, hdev).wait_send()


def local(velocity, kx_index, kz_index, helm_even, helm_odd, deriv_even, deriv_odd):
    v = velocity.reshape(NZ, NB, NC * NL)
    vm = pl.BlockSpec(memory_space=pltpu.VMEM)
    hbm = pl.BlockSpec(memory_space=pl.ANY)
    shape = jax.ShapeDtypeStruct((NZ, NB, NC * NL), jnp.bfloat16)
    dma = pltpu.SemaphoreType.DMA
    outu, outd = pl.pallas_call(
        kernel,
        out_shape=(shape, shape),
        in_specs=[hbm, pl.BlockSpec(memory_space=pltpu.SMEM), vm, hbm, hbm, hbm, hbm],
        out_specs=(vm, vm),
        scratch_shapes=[
            pltpu.VMEM((NC, NZ, NB, NL), jnp.bfloat16),
            pltpu.VMEM((NC, NX * NZ, NB, NL), jnp.bfloat16),
            pltpu.VMEM((NC, 2, NZ, NB, NL), jnp.bfloat16),
            pltpu.VMEM((NC, 2, NZ, NB, NL), jnp.bfloat16),
            pltpu.VMEM((HALF, HALF), jnp.bfloat16),
            pltpu.VMEM((HALF, HALF), jnp.bfloat16),
            pltpu.VMEM((OWN, HALF), jnp.bfloat16),
            pltpu.VMEM((OWN, HALF), jnp.bfloat16),
            pltpu.VMEM((8, 1, NL), jnp.float32),
            pltpu.VMEM((NX, 1, NL), jnp.float32),
            pltpu.VMEM((2, 1, NL), jnp.float32),
            pltpu.VMEM((NZ, 1, NL), jnp.float32),
            dma((NC,)), dma((4,)),
            dma((NC, NZ)), dma((NC, NZ)),
            dma((NC, NX)), dma((NC, NX)),
            dma((NC, 2, NZ)), dma((NC, 2, NZ)),
            dma((8,)), dma((8,)), dma((NX,)), dma((NX,)), dma((1,)), dma((2,)), dma((NZ,)), dma((NZ,)),
        ],
        compiler_params=pltpu.CompilerParams(collective_id=0, has_side_effects=True),
    )(v, kx_index, kz_index.reshape(1, NC * NL), helm_even, helm_odd, deriv_even, deriv_odd)
    full = (2, KX, NB, NC * NL)
    return outu.reshape(full), outd.reshape(full)


def solution(mesh):
    in_specs = (P(None, None, "wall", "span"), P(), P("span"), P(), P(), P(), P())
    out_specs = (P(None, None, "wall", "span"), P(None, None, "wall", "span"))
    return jax.shard_map(local, mesh=mesh, in_specs=in_specs, out_specs=out_specs, check_vma=False)
```

```python
import jax
import jax.numpy as jnp
from jax import lax
from jax.experimental import pallas as pl
from jax.experimental.pallas import tpu as pltpu
from jax.sharding import PartitionSpec as P

NY = 1536
KZ = 4096
XMODES = 5120
KX = 8
HALF = NY // 2
NX = 4
NZ = 16
NQ = 16
NJ = NZ // NQ
NG = 8
NB = 24
NL = 128
NC = 2
OWN = NQ * NB
NR = NJ * NC
MESH = pl.DeviceIdType.MESH
f32, bf16 = jnp.float32, jnp.bfloat16


def kernel(
    v_hbm, kx_ref, kz_ref, he_hbm, ho_hbm, de_hbm, do_hbm,
    outu_ref, outd_ref,
    v_scr, rx, tx, rxo, he, ho, de, do, hes, hos, e1, e2, e3, e4,
    loc_sem, w_sem, entered, zs, zr, xs, xr, bs, br, es1, er1, es2, er2, es3, er3, es4, er4,
):
    wall = lax.axis_index("wall")
    span = lax.axis_index("span")
    x, z = wall // NZ, wall % NZ
    yy, zh, core = span // 4, (span // 2) % 2, span % 2
    yc = yy * 2 + core
    half = z // NQ

    def at_z(p):
        return (x * NZ + p, span)

    def at_x(d):
        return (((x + d) % NX) * NZ + z, span)

    def at_yc(d):
        t = (yc + d) % 8
        return (wall, ((t // 2) * 2 + zh) * 2 + t % 2)

    across = (x * NZ + (NZ - 1 - z), (yy * 2 + (1 - zh)) * 2 + core)

    vcopies = [
        pltpu.make_async_copy(v_hbm.at[:, :, pl.ds(h * NL, NL)], v_scr.at[:, h], loc_sem.at[h]) for h in range(NC)
    ]
    m = x // 2
    plane0 = NZ * NB * x + OWN * half
    i0 = (1 - m) * plane0 + m * (NY - OWN - plane0)
    i0 = pl.multiple_of(i0, OWN)
    wcopies = [
        pltpu.make_async_copy(he_hbm, he, w_sem.at[0]),
        pltpu.make_async_copy(ho_hbm, ho, w_sem.at[1]),
        pltpu.make_async_copy(de_hbm.at[pl.ds(i0, OWN), :], de, w_sem.at[2]),
        pltpu.make_async_copy(do_hbm.at[pl.ds(i0, OWN), :], do, w_sem.at[3]),
    ]

    barrier = pltpu.get_barrier_semaphore()

    def greet(dev):
        pl.semaphore_signal(barrier, inc=1, device_id=dev, device_id_type=MESH)

    def greet_up(p, carry):
        greet(at_z(p))
        return carry

    lax.fori_loop(z + 1, NZ, greet_up, 0)

    @pl.when(zh == 0)
    def _():
        greet(across)

    for d in range(1, NX):
        greet(at_x(d))
    for d in range(1, 8):
        greet(at_yc(d))
    for c in vcopies + wcopies:
        c.start()

    for c in vcopies:
        c.wait()
    part = jnp.zeros((8, NL), f32)
    for c in range(NZ):
        for h in range(NC):
            w = v_scr[c, h].astype(f32)
            w = w * w
            part = part + (w[0:8] + w[8:16] + w[16:24])
    e1[yc] = jnp.sum(part, axis=0, keepdims=True)

    pl.semaphore_wait(barrier, z + zh + (NX - 1) + 7)

    def zcopy(r, p):
        j, h = r // NC, r % NC
        return pltpu.make_async_remote_copy(
            src_ref=v_scr.at[NJ * (p % NQ) + j, h], dst_ref=rx.at[r, x * NZ + z],
            send_sem=zs.at[r, p], recv_sem=zr.at[r, z],
            device_id=at_z(p), device_id_type=MESH,
        )

    def zwait(r, q):
        pltpu.make_async_remote_copy(
            src_ref=v_scr.at[0, 0], dst_ref=rx.at[r, x * NZ + q],
            send_sem=zs.at[r, q], recv_sem=zr.at[r, q],
            device_id=across, device_id_type=MESH,
        ).wait_recv()

    def tell(i, carry):
        pl.semaphore_signal(entered.at[z], inc=1, device_id=at_z(z - 1 - i), device_id_type=MESH)
        return carry

    lax.fori_loop(0, z, tell, 0)

    @pl.when(zh == 1)
    def _():
        pl.semaphore_signal(entered.at[NZ], inc=1, device_id=across, device_id_type=MESH)

    for r in range(NR):
        lax.fori_loop(0, z, lambda p, c, r=r: (zcopy(r, p).start(), c)[1], 0)

    def ecopy(buf, slot, ss, rs, dev):
        return pltpu.make_async_remote_copy(
            src_ref=buf.at[slot], dst_ref=buf.at[slot], send_sem=ss, recv_sem=rs,
            device_id=dev, device_id_type=MESH,
        )

    for d in range(1, 8):
        ecopy(e1, yc, es1.at[d], er1.at[yc], at_yc(d)).start()

    for d in range(1, 8):
        ecopy(e1, (yc + d) % 8, es1.at[d], er1.at[(yc + d) % 8], across).wait_recv()
    e2[x] = jnp.sum(e1[...], axis=0)
    for d in range(1, NX):
        ecopy(e2, x, es2.at[d], er2.at[x], at_x(d)).start()
    for d in range(1, NX):
        ecopy(e2, (x + d) % NX, es2.at[d], er2.at[(x + d) % NX], across).wait_recv()
    e3[zh] = jnp.sum(e2[...], axis=0)

    @pl.when(zh == 1)
    def _():
        ecopy(e3, zh, es3.at[0], er3.at[zh], across).start()

    def send_up(p, carry):
        pl.semaphore_wait(entered.at[p], 1)
        for r in range(NR // 2):
            zcopy(r, p).start()
        return carry

    lax.fori_loop(z + 1, NZ, send_up, 0)
    for r in range(NR // 2, NR):
        lax.fori_loop(0, NZ - 1 - z, lambda i, c, r=r: (zcopy(r, NZ - 1 - i).start(), c)[1], 0)
    for r in range(NR):
        pltpu.make_async_copy(v_scr.at[NJ * (z % NQ) + r // NC, r % NC], rx.at[r, x * NZ + z], zr.at[r, z]).start()

    @pl.when(zh == 0)
    def _():
        pl.semaphore_wait(entered.at[NZ], 1)
        ecopy(e3, zh, es3.at[0], er3.at[zh], across).start()

    rows = lax.broadcasted_iota(jnp.int32, (256, 256), 0)
    cols = lax.broadcasted_iota(jnp.int32, (256, 256), 1)
    flip256 = jnp.where(rows + cols == 255, 1.0, 0.0).astype(bf16)
    rows = lax.broadcasted_iota(jnp.int32, (OWN, OWN), 0)
    cols = lax.broadcasted_iota(jnp.int32, (OWN, OWN), 1)
    flip_own = jnp.where(rows + cols == OWN - 1, 1.0, 0.0).astype(bf16)
    mirrored = x >= 2
    sign = jnp.where(mirrored, -1.0, 1.0).astype(f32)

    def group(g):
        return ((z // NG + g) % 2) * NG

    def xcopy(r, g, d):
        blocks = pl.ds(x * NZ + group(g), NG)
        return pltpu.make_async_remote_copy(
            src_ref=rx.at[r, blocks], dst_ref=rx.at[r, blocks],
            send_sem=xs.at[r, g, d], recv_sem=xr.at[r, g, d],
            device_id=at_x(d), device_id_type=MESH,
        )

    def xwait(r, g, d):
        blocks = pl.ds(((x + NX - d) % NX) * NZ + group(g), NG)
        pltpu.make_async_remote_copy(
            src_ref=rx.at[r, blocks], dst_ref=rx.at[r, blocks],
            send_sem=xs.at[r, g, d], recv_sem=xr.at[r, g, d],
            device_id=at_x(d), device_id_type=MESH,
        ).wait_recv()

    def bcopy(r, d):
        p = (z + d) % NQ
        return pltpu.make_async_remote_copy(
            src_ref=tx.at[r, p], dst_ref=rxo.at[r, z % NQ],
            send_sem=bs.at[r, d], recv_sem=br.at[r, z % NQ],
            device_id=at_z(half * NQ + p), device_id_type=MESH,
        )

    def compute(r):
        lo = rx[r, 0:32].astype(f32).reshape(HALF, NL)
        hi = rx[r, 32:64].astype(f32).reshape(HALF, NL).astype(bf16)
        fl = jnp.concatenate(
            [jnp.dot(flip256, hi[HALF - 256 * (b + 1):HALF - 256 * b], preferred_element_type=f32) for b in range(3)],
            axis=0,
        )
        even = ((lo + fl) * 0.5).astype(bf16)
        odd = ((lo - fl) * 0.5).astype(bf16)
        heven = jnp.dot(he[...], even, preferred_element_type=f32).astype(bf16)
        hodd = jnp.dot(ho[...], odd, preferred_element_type=f32).astype(bf16)
        hes[...] = heven
        hos[...] = hodd
        dodd = jnp.dot(de[...], heven, preferred_element_type=f32)
        deven = jnp.dot(do[...], hodd, preferred_element_type=f32)
        he32 = hes[pl.ds(i0, OWN), :].astype(f32)
        ho32 = hos[pl.ds(i0, OWN), :].astype(f32)

        def place(t, lines):
            back = jnp.dot(flip_own, lines, preferred_element_type=f32)
            res = jnp.where(mirrored, back, lines.astype(f32))
            tx[r, :, t] = res.reshape(NQ, NB, NL).astype(bf16)

        place(0, (he32 + sign * ho32).astype(bf16))
        place(1, (deven + sign * dodd).astype(bf16))

    for r in range(NR):
        for g in range(2):
            lax.fori_loop(0, NG, lambda q, c, g=g: (zwait(r, group(g) + q), c)[1], 0)
            for d in range(1, NX):
                xcopy(r, g, d).start()
        if r == 0:
            for c in wcopies:
                c.wait()
            ecopy(e3, 1 - zh, es3.at[0], er3.at[1 - zh], across).wait_recv()
            e4[z] = jnp.sum(e3[...], axis=0)

            def send_e4(d, carry):
                ecopy(e4, z, es4.at[d], er4.at[z], at_z((z + d) % NZ)).start()
                return carry

            lax.fori_loop(1, NZ, send_e4, 0)
        for g in range(2):
            for d in range(1, NX):
                xwait(r, g, d)
        compute(r)

        def send_back(i, carry):
            bcopy(r, NQ // 2 - i).start()

            @pl.when(i > 0)
            def _():
                bcopy(r, NQ // 2 + i).start()
            return carry

        lax.fori_loop(0, NQ // 2, send_back, 0)
        pltpu.make_async_copy(tx.at[r, z % NQ], rxo.at[r, z % NQ], br.at[r, z % NQ]).start()

    kz = kz_ref[...].astype(f32) / KZ
    kz_sq = kz * kz

    def wait_e4(d, carry):
        p = (z + d) % NZ
        ecopy(e4, p, es4.at[d], er4.at[p], across).wait_recv()
        return carry

    lax.fori_loop(1, NZ, wait_e4, 0)
    energy = jnp.sum(jnp.sum(e4[...], axis=0), axis=1, keepdims=True)
    scale = jnp.float32(2.0 * KX * NY * KZ) / energy
    factors = []
    for k in range(KX):
        kx = kx_ref[k].astype(f32) / XMODES
        factors.append(scale * (1.0 / (1.0 + 2.0 * (kx * kx + kz_sq))))

    def bwait(r, q):
        pltpu.make_async_remote_copy(
            src_ref=tx.at[r, q], dst_ref=rxo.at[r, q],
            send_sem=bs.at[r, 0], recv_sem=br.at[r, q],
            device_id=across, device_id_type=MESH,
        ).wait_recv()

    for r in range(NR):
        j, h = r // NC, r % NC
        lax.fori_loop(0, NQ, lambda q, carry: (bwait(r, q), carry)[1], 0)
        for q in range(NQ):
            c = NJ * q + j
            f = factors[c % KX][:, h * NL:(h + 1) * NL]
            for t, out in enumerate((outu_ref, outd_ref)):
                out[c, :, h * NL:(h + 1) * NL] = (f * rxo[r, q, t].astype(f32)).astype(bf16)

    def drain_z(d, carry):
        for r in range(NR):
            zcopy(r, (z + d) % NZ).wait_send()
        return carry

    lax.fori_loop(1, NZ, drain_z, 0)

    def drain_b(d, carry):
        for r in range(NR):
            bcopy(r, d).wait_send()
        return carry

    lax.fori_loop(1, NQ, drain_b, 0)
    for d in range(1, NX):
        for r in range(NR):
            for g in range(2):
                xcopy(r, g, d).wait_send()
        ecopy(e2, x, es2.at[d], er2.at[x], at_x(d)).wait_send()
    for d in range(1, 8):
        ecopy(e1, yc, es1.at[d], er1.at[yc], at_yc(d)).wait_send()

    ecopy(e3, zh, es3.at[0], er3.at[zh], across).wait_send()

    def drain_e4(d, carry):
        ecopy(e4, z, es4.at[d], er4.at[z], at_z((z + d) % NZ)).wait_send()
        return carry

    lax.fori_loop(1, NZ, drain_e4, 0)


def local(velocity, kx_index, kz_index, helm_even, helm_odd, deriv_even, deriv_odd):
    v = velocity.reshape(NZ, NB, NC * NL)
    vm = pl.BlockSpec(memory_space=pltpu.VMEM)
    hbm = pl.BlockSpec(memory_space=pl.ANY)
    shape = jax.ShapeDtypeStruct((NZ, NB, NC * NL), bf16)
    dma = pltpu.SemaphoreType.DMA
    outu, outd = pl.pallas_call(
        kernel,
        out_shape=(shape, shape),
        in_specs=[hbm, pl.BlockSpec(memory_space=pltpu.SMEM), vm, hbm, hbm, hbm, hbm],
        out_specs=(vm, vm),
        scratch_shapes=[
            pltpu.VMEM((NZ, NC, NB, NL), bf16),
            pltpu.VMEM((NR, NX * NZ, NB, NL), bf16),
            pltpu.VMEM((NR, NQ, 2, NB, NL), bf16),
            pltpu.VMEM((NR, NQ, 2, NB, NL), bf16),
            pltpu.VMEM((HALF, HALF), bf16),
            pltpu.VMEM((HALF, HALF), bf16),
            pltpu.VMEM((OWN, HALF), bf16),
            pltpu.VMEM((OWN, HALF), bf16),
            pltpu.VMEM((HALF, NL), bf16),
            pltpu.VMEM((HALF, NL), bf16),
            pltpu.VMEM((8, 1, NL), f32),
            pltpu.VMEM((NX, 1, NL), f32),
            pltpu.VMEM((2, 1, NL), f32),
            pltpu.VMEM((NZ, 1, NL), f32),
            dma((NC,)), dma((4,)), pltpu.SemaphoreType.REGULAR((NZ + 1,)),
            dma((NR, NZ)), dma((NR, NZ)),
            dma((NR, 2, NX)), dma((NR, 2, NX)),
            dma((NR, NQ)), dma((NR, NQ)),
            dma((8,)), dma((8,)), dma((NX,)), dma((NX,)),
            dma((1,)), dma((2,)), dma((NZ,)), dma((NZ,)),
        ],
        compiler_params=pltpu.CompilerParams(collective_id=0, has_side_effects=True),
    )(v, kx_index, kz_index.reshape(1, NC * NL), helm_even, helm_odd, deriv_even, deriv_odd)
    full = (2, KX, NB, NC * NL)
    return outu.reshape(full), outd.reshape(full)


def solution(mesh):
    in_specs = (P(None, None, "wall", "span"), P(), P("span"), P(), P(), P(), P())
    out_specs = (P(None, None, "wall", "span"), P(None, None, "wall", "span"))
    return jax.shard_map(local, mesh=mesh, in_specs=in_specs, out_specs=out_specs, check_vma=False)
```

```python
import jax
import jax.numpy as jnp
from jax import lax
from jax.experimental import pallas as pl
from jax.experimental.pallas import tpu as pltpu
from jax.sharding import PartitionSpec as P

NY = 1536
KZ = 4096
XMODES = 5120
KX = 8
HALF = NY // 2
NX = 4
NZ = 16
NG = 4
NLATE = 2
E0 = 4
NB = 24
NL = 128
NC = 2
OWN = NZ * NB
NR = NC
NE = NLATE * NC
MESH = pl.DeviceIdType.MESH
f32, bf16 = jnp.float32, jnp.bfloat16


def kernel(
    v_hbm, kx_ref, kz_ref, he_hbm, ho_hbm, de_hbm, do_hbm,
    outu_ref, outd_ref,
    v_scr, rx, tx, rxo, he, ho, de, do, hes, hos, e1, e2, e3, e4,
    loc_sem, w_sem, entered, zs, zr, xs, xr, bs, br, es1, er1, es2, er2, es3, er3, es4, er4,
):
    wall = lax.axis_index("wall")
    span = lax.axis_index("span")
    x, z = wall // NZ, wall % NZ
    yy, zh, core = span // 4, (span // 2) % 2, span % 2
    yc = yy * 2 + core
    n_own = NZ - NLATE * (1 - zh)
    owner = z < n_own
    extra = (zh == 0) & (z >= E0) & (z < E0 + NE)

    def at_z(p):
        return (x * NZ + p, span)

    def at_x(d):
        return (((x + d) % NX) * NZ + z, span)

    def at_yc(d):
        t = (yc + d) % 8
        return (wall, ((t // 2) * 2 + zh) * 2 + t % 2)

    across = (x * NZ + (NZ - 1 - z), (yy * 2 + (1 - zh)) * 2 + core)

    vcopies = [
        pltpu.make_async_copy(v_hbm.at[:, :, pl.ds(h * NL, NL)], v_scr.at[:, h], loc_sem.at[h]) for h in range(NC)
    ]
    m = x // 2
    plane0 = OWN * x
    i0 = (1 - m) * plane0 + m * (NY - OWN - plane0)
    i0 = pl.multiple_of(i0, OWN)
    wcopies = [
        pltpu.make_async_copy(he_hbm, he, w_sem.at[0]),
        pltpu.make_async_copy(ho_hbm, ho, w_sem.at[1]),
        pltpu.make_async_copy(de_hbm.at[pl.ds(i0, OWN), :], de, w_sem.at[2]),
        pltpu.make_async_copy(do_hbm.at[pl.ds(i0, OWN), :], do, w_sem.at[3]),
    ]

    barrier = pltpu.get_barrier_semaphore()

    def greet(dev):
        pl.semaphore_signal(barrier, inc=1, device_id=dev, device_id_type=MESH)

    def greet_up(p, carry):
        greet(at_z(p))
        return carry

    lax.fori_loop(z + 1, NZ, greet_up, 0)

    @pl.when(zh == 0)
    def _():
        greet(across)

    for d in range(1, NX):
        greet(at_x(d))
    for d in range(1, 8):
        greet(at_yc(d))
    for c in vcopies + wcopies:
        c.start()

    for c in vcopies:
        c.wait()
    part = jnp.zeros((8, NL), f32)
    for c in range(NZ):
        for h in range(NC):
            w = v_scr[c, h].astype(f32)
            w = w * w
            part = part + (w[0:8] + w[8:16] + w[16:24])
    e1[yc] = jnp.sum(part, axis=0, keepdims=True)

    pl.semaphore_wait(barrier, z + zh + (NX - 1) + 7)

    def block(r, p):
        if r < NR:
            return p, r
        t = p - E0
        return NZ - NLATE + t // NC, t % NC

    def zcopy(r, p):
        c, h = block(r, p)
        return pltpu.make_async_remote_copy(
            src_ref=v_scr.at[c, h], dst_ref=rx.at[r, x * NZ + z],
            send_sem=zs.at[r, p], recv_sem=zr.at[r, z],
            device_id=at_z(p), device_id_type=MESH,
        )

    def zwait(r, q):
        pltpu.make_async_remote_copy(
            src_ref=v_scr.at[0, 0], dst_ref=rx.at[r, x * NZ + q],
            send_sem=zs.at[r, q], recv_sem=zr.at[r, q],
            device_id=across, device_id_type=MESH,
        ).wait_recv()

    def tell(i, carry):
        pl.semaphore_signal(entered.at[z], inc=1, device_id=at_z(z - 1 - i), device_id_type=MESH)
        return carry

    lax.fori_loop(0, z, tell, 0)

    @pl.when(zh == 1)
    def _():
        pl.semaphore_signal(entered.at[NZ], inc=1, device_id=across, device_id_type=MESH)

    def for_owners(r, do, below, far=False):
        if r < NR:
            first, end = (0, jnp.minimum(z, n_own)) if below else (z + 1, n_own)
        else:
            first, end = (E0, jnp.minimum(z, E0 + NE)) if below else (jnp.maximum(z + 1, E0), E0 + NE)
            end = jnp.where(zh == 0, end, first)

        def body(p, carry):
            do(end - 1 + first - p if far else p)
            return carry

        lax.fori_loop(first, end, body, 0)

    for r in range(NR + 1):
        for_owners(r, lambda p: zcopy(r, p).start(), True)

    def ecopy(buf, slot, ss, rs, dev):
        return pltpu.make_async_remote_copy(
            src_ref=buf.at[slot], dst_ref=buf.at[slot], send_sem=ss, recv_sem=rs,
            device_id=dev, device_id_type=MESH,
        )

    for d in range(1, 8):
        ecopy(e1, yc, es1.at[d], er1.at[yc], at_yc(d)).start()

    for d in range(1, 8):
        ecopy(e1, (yc + d) % 8, es1.at[d], er1.at[(yc + d) % 8], across).wait_recv()
    e2[x] = jnp.sum(e1[...], axis=0)
    for d in range(1, NX):
        ecopy(e2, x, es2.at[d], er2.at[x], at_x(d)).start()
    for d in range(1, NX):
        ecopy(e2, (x + d) % NX, es2.at[d], er2.at[(x + d) % NX], across).wait_recv()
    e3[zh] = jnp.sum(e2[...], axis=0)

    @pl.when(zh == 1)
    def _():
        ecopy(e3, zh, es3.at[0], er3.at[zh], across).start()

    def send_up(p, carry):
        pl.semaphore_wait(entered.at[p], 1)

        @pl.when(p < n_own)
        def _():
            zcopy(0, p).start()
        return carry

    lax.fori_loop(z + 1, NZ, send_up, 0)
    for r in range(1, NR + 1):
        for_owners(r, lambda p: zcopy(r, p).start(), False, True)

    rows = lax.broadcasted_iota(jnp.int32, (256, 256), 0)
    cols = lax.broadcasted_iota(jnp.int32, (256, 256), 1)
    flip256 = jnp.where(rows + cols == 255, 1.0, 0.0).astype(bf16)
    rows = lax.broadcasted_iota(jnp.int32, (OWN, OWN), 0)
    cols = lax.broadcasted_iota(jnp.int32, (OWN, OWN), 1)
    flip_own = jnp.where(rows + cols == OWN - 1, 1.0, 0.0).astype(bf16)
    mirrored = x >= 2
    sign = jnp.where(mirrored, -1.0, 1.0).astype(f32)

    def group(g):
        own, up = z // NG, z // NG // 2
        return (own, 1 - own + 4 * up, 2 - up, 3 - 3 * up)[g] * NG

    def xcopy(r, g, d):
        blocks = pl.ds(x * NZ + group(g), NG)
        return pltpu.make_async_remote_copy(
            src_ref=rx.at[r, blocks], dst_ref=rx.at[r, blocks],
            send_sem=xs.at[r, g, d], recv_sem=xr.at[r, g, d],
            device_id=at_x(d), device_id_type=MESH,
        )

    def xwait(r, g, d):
        blocks = pl.ds(((x + NX - d) % NX) * NZ + group(g), NG)
        pltpu.make_async_remote_copy(
            src_ref=rx.at[r, blocks], dst_ref=rx.at[r, blocks],
            send_sem=xs.at[r, g, d], recv_sem=xr.at[r, g, d],
            device_id=at_x(d), device_id_type=MESH,
        ).wait_recv()

    def bcopy(r, p):
        c, h = block(r, z)
        return pltpu.make_async_remote_copy(
            src_ref=tx.at[r, p], dst_ref=rxo.at[h, c],
            send_sem=bs.at[r, p], recv_sem=br.at[h, c],
            device_id=at_z(p), device_id_type=MESH,
        )

    def compute(r):
        lo = rx[r, 0:32].astype(f32).reshape(HALF, NL)
        hi = rx[r, 32:64].astype(f32).reshape(HALF, NL).astype(bf16)
        fl = jnp.concatenate(
            [jnp.dot(flip256, hi[HALF - 256 * (b + 1):HALF - 256 * b], preferred_element_type=f32) for b in range(3)],
            axis=0,
        )
        even = ((lo + fl) * 0.5).astype(bf16)
        odd = ((lo - fl) * 0.5).astype(bf16)
        heven = jnp.dot(he[...], even, preferred_element_type=f32).astype(bf16)
        hodd = jnp.dot(ho[...], odd, preferred_element_type=f32).astype(bf16)
        hes[...] = heven
        hos[...] = hodd
        dodd = jnp.dot(de[...], heven, preferred_element_type=f32)
        deven = jnp.dot(do[...], hodd, preferred_element_type=f32)
        he32 = hes[pl.ds(i0, OWN), :].astype(f32)
        ho32 = hos[pl.ds(i0, OWN), :].astype(f32)

        def place(t, lines):
            back = jnp.dot(flip_own, lines, preferred_element_type=f32)
            res = jnp.where(mirrored, back, lines.astype(f32))
            tx[r, :, t] = res.reshape(NZ, NB, NL).astype(bf16)

        place(0, (he32 + sign * ho32).astype(bf16))
        place(1, (deven + sign * dodd).astype(bf16))

    def energy_on():
        @pl.when(zh == 0)
        def _():
            pl.semaphore_wait(entered.at[NZ], 1)
            ecopy(e3, zh, es3.at[0], er3.at[zh], across).start()

        ecopy(e3, 1 - zh, es3.at[0], er3.at[1 - zh], across).wait_recv()
        e4[z] = jnp.sum(e3[...], axis=0)

        def send_e4(d, carry):
            ecopy(e4, z, es4.at[d], er4.at[z], at_z((z + d) % NZ)).start()
            return carry

        lax.fori_loop(1, NZ, send_e4, 0)

    def round_of(r):
        c, h = block(r, z)
        pltpu.make_async_copy(v_scr.at[c, h], rx.at[r, x * NZ + z], zr.at[r, z]).start()
        for g in range(NZ // NG):
            lax.fori_loop(0, NG, lambda q, cc, g=g: (zwait(r, group(g) + q), cc)[1], 0)
            for d in range(1, NX):
                xcopy(r, g, d).start()
        if r == 0:
            for w in wcopies:
                w.wait()
        for g in range(NZ // NG):
            for d in range(1, NX):
                xwait(r, g, d)
        compute(r)

        def send_back(i, carry):
            k = NZ - 1 - i

            @pl.when(z >= k)
            def _():
                bcopy(r, z - k).start()

            @pl.when(z + k < NZ)
            def _():
                bcopy(r, z + k).start()
            return carry

        lax.fori_loop(0, NZ - 1, send_back, 0)
        pltpu.make_async_copy(tx.at[r, z], rxo.at[h, c], br.at[h, c]).start()

    @pl.when(owner)
    def _():
        round_of(0)
        energy_on()
        round_of(1)

    @pl.when(extra)
    def _():
        round_of(NR)

    @pl.when(jnp.logical_not(owner))
    def _():
        for w in wcopies:
            w.wait()
        energy_on()

    kz = kz_ref[...].astype(f32) / KZ
    kz_sq = kz * kz

    def wait_e4(d, carry):
        p = (z + d) % NZ
        ecopy(e4, p, es4.at[d], er4.at[p], across).wait_recv()
        return carry

    lax.fori_loop(1, NZ, wait_e4, 0)
    energy = jnp.sum(jnp.sum(e4[...], axis=0), axis=1, keepdims=True)
    scale = jnp.float32(2.0 * KX * NY * KZ) / energy
    factors = []
    for k in range(KX):
        kx = kx_ref[k].astype(f32) / XMODES
        factors.append(scale * (1.0 / (1.0 + 2.0 * (kx * kx + kz_sq))))

    def bwait(r, q):
        pltpu.make_async_remote_copy(
            src_ref=tx.at[r, q], dst_ref=rxo.at[r, q],
            send_sem=bs.at[r, 0], recv_sem=br.at[r, q],
            device_id=across, device_id_type=MESH,
        ).wait_recv()

    for r in range(NR):
        h = r
        lax.fori_loop(0, NZ, lambda q, carry: (bwait(r, q), carry)[1], 0)
        for q in range(NZ):
            c = q
            f = factors[c % KX][:, h * NL:(h + 1) * NL]
            for t, out in enumerate((outu_ref, outd_ref)):
                out[c, :, h * NL:(h + 1) * NL] = (f * rxo[r, q, t].astype(f32)).astype(bf16)

    for r in range(NR + 1):
        for_owners(r, lambda p: zcopy(r, p).wait_send(), True)
        for_owners(r, lambda p: zcopy(r, p).wait_send(), False)

    def drain_round(r):
        lax.fori_loop(1, NZ, lambda d, cc: (bcopy(r, (z + d) % NZ).wait_send(), cc)[1], 0)
        for d in range(1, NX):
            for g in range(NZ // NG):
                xcopy(r, g, d).wait_send()

    @pl.when(owner)
    def _():
        for r in range(NR):
            drain_round(r)

    @pl.when(extra)
    def _():
        drain_round(NR)

    for d in range(1, NX):
        ecopy(e2, x, es2.at[d], er2.at[x], at_x(d)).wait_send()
    for d in range(1, 8):
        ecopy(e1, yc, es1.at[d], er1.at[yc], at_yc(d)).wait_send()

    ecopy(e3, zh, es3.at[0], er3.at[zh], across).wait_send()

    def drain_e4(d, carry):
        ecopy(e4, z, es4.at[d], er4.at[z], at_z((z + d) % NZ)).wait_send()
        return carry

    lax.fori_loop(1, NZ, drain_e4, 0)


def settle(u_ref, d_ref, outu_ref, outd_ref, sem):
    copies = [
        pltpu.make_async_copy(u_ref, outu_ref, sem.at[0]),
        pltpu.make_async_copy(d_ref, outd_ref, sem.at[1]),
    ]
    for c in copies:
        c.start()
    for c in copies:
        c.wait()


def local(velocity, kx_index, kz_index, helm_even, helm_odd, deriv_even, deriv_odd):
    v = velocity.reshape(NZ, NB, NC * NL)
    vm = pl.BlockSpec(memory_space=pltpu.VMEM)
    hbm = pl.BlockSpec(memory_space=pl.ANY)
    shape = jax.ShapeDtypeStruct((NZ, NB, NC * NL), bf16)
    dma = pltpu.SemaphoreType.DMA
    outu, outd = pl.pallas_call(
        kernel,
        out_shape=(pltpu.VMEM((NZ, NB, NC * NL), bf16),) * 2,
        in_specs=[hbm, pl.BlockSpec(memory_space=pltpu.SMEM), vm, hbm, hbm, hbm, hbm],
        out_specs=(vm, vm),
        scratch_shapes=[
            pltpu.VMEM((NZ, NC, NB, NL), bf16),
            pltpu.VMEM((NR + 1, NX * NZ, NB, NL), bf16),
            pltpu.VMEM((NR + 1, NZ, 2, NB, NL), bf16),
            pltpu.VMEM((NR, NZ, 2, NB, NL), bf16),
            pltpu.VMEM((HALF, HALF), bf16),
            pltpu.VMEM((HALF, HALF), bf16),
            pltpu.VMEM((OWN, HALF), bf16),
            pltpu.VMEM((OWN, HALF), bf16),
            pltpu.VMEM((HALF, NL), bf16),
            pltpu.VMEM((HALF, NL), bf16),
            pltpu.VMEM((8, 1, NL), f32),
            pltpu.VMEM((NX, 1, NL), f32),
            pltpu.VMEM((2, 1, NL), f32),
            pltpu.VMEM((NZ, 1, NL), f32),
            dma((NC,)), dma((4,)), pltpu.SemaphoreType.REGULAR((NZ + 1,)),
            dma((NR + 1, NZ)), dma((NR + 1, NZ)),
            dma((NR + 1, NZ // NG, NX)), dma((NR + 1, NZ // NG, NX)),
            dma((NR + 1, NZ)), dma((NR, NZ)),
            dma((8,)), dma((8,)), dma((NX,)), dma((NX,)),
            dma((1,)), dma((2,)), dma((NZ,)), dma((NZ,)),
        ],
        compiler_params=pltpu.CompilerParams(collective_id=0, has_side_effects=True),
    )(v, kx_index, kz_index.reshape(1, NC * NL), helm_even, helm_odd, deriv_even, deriv_odd)
    outu, outd = pl.pallas_call(
        settle, out_shape=(shape, shape), in_specs=[hbm, hbm], out_specs=(hbm, hbm),
        scratch_shapes=[dma((2,))], compiler_params=pltpu.CompilerParams(vmem_limit_bytes=2 ** 20),
    )(outu, outd)
    full = (2, KX, NB, NC * NL)
    return outu.reshape(full), outd.reshape(full)


def solution(mesh):
    in_specs = (P(None, None, "wall", "span"), P(), P("span"), P(), P(), P(), P())
    out_specs = (P(None, None, "wall", "span"), P(None, None, "wall", "span"))
    return jax.shard_map(local, mesh=mesh, in_specs=in_specs, out_specs=out_specs, check_vma=False)
```

```python
import jax
import jax.numpy as jnp
from jax import lax
from jax.experimental import pallas as pl
from jax.experimental.pallas import tpu as pltpu
from jax.sharding import PartitionSpec as P

NY = 1536
KZ = 4096
XMODES = 5120
KX = 8
HALF = NY // 2
NX = 4
NZ = 16
NG = 4
NLATE = 2
E0 = 5
NB = 24
NL = 128
NC = 2
OWN = NZ * NB
NR = NC
NE = NLATE * NC
MESH = pl.DeviceIdType.MESH
f32, bf16 = jnp.float32, jnp.bfloat16


def kernel(
    v_hbm, kx_ref, kz_ref, he_hbm, ho_hbm, de_hbm, do_hbm,
    outu_ref, outd_ref,
    v_scr, rx, tx, rxo, he, ho, de, do, hes, hos, e1, e2, e3, e4,
    loc_sem, w_sem, entered, zs, zr, xs, xr, bs, br, es1, er1, es2, er2, es3, er3, es4, er4,
):
    wall = lax.axis_index("wall")
    span = lax.axis_index("span")
    x, z = wall // NZ, wall % NZ
    yy, zh, core = span // 4, (span // 2) % 2, span % 2
    yc = yy * 2 + core
    n_own = NZ - NLATE * (1 - zh)
    owner = z < n_own
    extra = (zh == 0) & (z >= E0) & (z < E0 + NE)

    def at_z(p):
        return (x * NZ + p, span)

    def at_x(d):
        return (((x + d) % NX) * NZ + z, span)

    def at_yc(d):
        t = (yc + d) % 8
        return (wall, ((t // 2) * 2 + zh) * 2 + t % 2)

    across = (x * NZ + (NZ - 1 - z), (yy * 2 + (1 - zh)) * 2 + core)

    vcopies = [
        pltpu.make_async_copy(v_hbm.at[:, :, pl.ds(h * NL, NL)], v_scr.at[:, h], loc_sem.at[h]) for h in range(NC)
    ]
    m = x // 2
    plane0 = OWN * x
    i0 = (1 - m) * plane0 + m * (NY - OWN - plane0)
    i0 = pl.multiple_of(i0, OWN)
    wcopies = [
        pltpu.make_async_copy(he_hbm, he, w_sem.at[0]),
        pltpu.make_async_copy(ho_hbm, ho, w_sem.at[1]),
        pltpu.make_async_copy(de_hbm.at[pl.ds(i0, OWN), :], de, w_sem.at[2]),
        pltpu.make_async_copy(do_hbm.at[pl.ds(i0, OWN), :], do, w_sem.at[3]),
    ]

    barrier = pltpu.get_barrier_semaphore()

    def greet(dev):
        pl.semaphore_signal(barrier, inc=1, device_id=dev, device_id_type=MESH)

    def greet_up(p, carry):
        greet(at_z(p))
        return carry

    lax.fori_loop(z + 1, NZ, greet_up, 0)

    @pl.when(zh == 0)
    def _():
        greet(across)

    for d in range(1, NX):
        greet(at_x(d))
    for d in range(1, 8):
        greet(at_yc(d))
    for c in vcopies + wcopies:
        c.start()

    for c in vcopies:
        c.wait()
    part = jnp.zeros((8, NL), f32)
    for c in range(NZ):
        for h in range(NC):
            w = v_scr[c, h].astype(f32)
            w = w * w
            part = part + (w[0:8] + w[8:16] + w[16:24])
    e1[yc] = jnp.sum(part, axis=0, keepdims=True)

    pl.semaphore_wait(barrier, z + zh + (NX - 1) + 7)

    def block(r, p):
        if r < NR:
            return p, r
        t = p - E0
        return NZ - NLATE + t // NC, t % NC

    def zcopy(r, p):
        c, h = block(r, p)
        return pltpu.make_async_remote_copy(
            src_ref=v_scr.at[c, h], dst_ref=rx.at[r, x * NZ + z],
            send_sem=zs.at[r, p], recv_sem=zr.at[r, z],
            device_id=at_z(p), device_id_type=MESH,
        )

    def zwait(r, q):
        pltpu.make_async_remote_copy(
            src_ref=v_scr.at[0, 0], dst_ref=rx.at[r, x * NZ + q],
            send_sem=zs.at[r, q], recv_sem=zr.at[r, q],
            device_id=across, device_id_type=MESH,
        ).wait_recv()

    def tell(i, carry):
        pl.semaphore_signal(entered.at[z], inc=1, device_id=at_z(z - 1 - i), device_id_type=MESH)
        return carry

    lax.fori_loop(0, z, tell, 0)

    @pl.when(zh == 1)
    def _():
        pl.semaphore_signal(entered.at[NZ], inc=1, device_id=across, device_id_type=MESH)

    def for_owners(r, do, below, far=False):
        if r < NR:
            first, end = (0, jnp.minimum(z, n_own)) if below else (z + 1, n_own)
        else:
            first, end = (E0, jnp.minimum(z, E0 + NE)) if below else (jnp.maximum(z + 1, E0), E0 + NE)
            end = jnp.where(zh == 0, end, first)

        def body(p, carry):
            do(end - 1 + first - p if far else p)
            return carry

        lax.fori_loop(first, end, body, 0)

    for r in range(NR + 1):
        for_owners(r, lambda p: zcopy(r, p).start(), True)

    def ecopy(buf, slot, ss, rs, dev):
        return pltpu.make_async_remote_copy(
            src_ref=buf.at[slot], dst_ref=buf.at[slot], send_sem=ss, recv_sem=rs,
            device_id=dev, device_id_type=MESH,
        )

    for d in range(1, 8):
        ecopy(e1, yc, es1.at[d], er1.at[yc], at_yc(d)).start()

    for d in range(1, 8):
        ecopy(e1, (yc + d) % 8, es1.at[d], er1.at[(yc + d) % 8], across).wait_recv()
    e2[x] = jnp.sum(e1[...], axis=0)
    for d in range(1, NX):
        ecopy(e2, x, es2.at[d], er2.at[x], at_x(d)).start()
    for d in range(1, NX):
        ecopy(e2, (x + d) % NX, es2.at[d], er2.at[(x + d) % NX], across).wait_recv()
    e3[zh] = jnp.sum(e2[...], axis=0)

    @pl.when(zh == 1)
    def _():
        ecopy(e3, zh, es3.at[0], er3.at[zh], across).start()

    def send_up(p, carry):
        pl.semaphore_wait(entered.at[p], 1)

        @pl.when(p < n_own)
        def _():
            zcopy(0, p).start()
        return carry

    lax.fori_loop(z + 1, NZ, send_up, 0)
    for r in range(1, NR + 1):
        for_owners(r, lambda p: zcopy(r, p).start(), False, True)

    rows = lax.broadcasted_iota(jnp.int32, (256, 256), 0)
    cols = lax.broadcasted_iota(jnp.int32, (256, 256), 1)
    flip256 = jnp.where(rows + cols == 255, 1.0, 0.0).astype(bf16)
    rows = lax.broadcasted_iota(jnp.int32, (OWN, OWN), 0)
    cols = lax.broadcasted_iota(jnp.int32, (OWN, OWN), 1)
    flip_own = jnp.where(rows + cols == OWN - 1, 1.0, 0.0).astype(bf16)
    mirrored = x >= 2
    sign = jnp.where(mirrored, -1.0, 1.0).astype(f32)

    def group(g):
        own, up = z // NG, z // NG // 2
        return (own, 1 - own + 4 * up, 2 - up, 3 - 3 * up)[g] * NG

    def xcopy(r, g, d):
        blocks = pl.ds(x * NZ + group(g), NG)
        return pltpu.make_async_remote_copy(
            src_ref=rx.at[r, blocks], dst_ref=rx.at[r, blocks],
            send_sem=xs.at[r, g, d], recv_sem=xr.at[r, g, d],
            device_id=at_x(d), device_id_type=MESH,
        )

    def xwait(r, g, d):
        blocks = pl.ds(((x + NX - d) % NX) * NZ + group(g), NG)
        pltpu.make_async_remote_copy(
            src_ref=rx.at[r, blocks], dst_ref=rx.at[r, blocks],
            send_sem=xs.at[r, g, d], recv_sem=xr.at[r, g, d],
            device_id=at_x(d), device_id_type=MESH,
        ).wait_recv()

    def bcopy(r, p):
        c, h = block(r, z)
        return pltpu.make_async_remote_copy(
            src_ref=tx.at[r, p], dst_ref=rxo.at[h, c],
            send_sem=bs.at[r, p], recv_sem=br.at[h, c],
            device_id=at_z(p), device_id_type=MESH,
        )

    def compute(r):
        lo = rx[r, 0:32].astype(f32).reshape(HALF, NL)
        hi = rx[r, 32:64].astype(f32).reshape(HALF, NL).astype(bf16)
        fl = jnp.concatenate(
            [jnp.dot(flip256, hi[HALF - 256 * (b + 1):HALF - 256 * b], preferred_element_type=f32) for b in range(3)],
            axis=0,
        )
        even = ((lo + fl) * 0.5).astype(bf16)
        odd = ((lo - fl) * 0.5).astype(bf16)
        heven = jnp.dot(he[...], even, preferred_element_type=f32).astype(bf16)
        hodd = jnp.dot(ho[...], odd, preferred_element_type=f32).astype(bf16)
        hes[...] = heven
        hos[...] = hodd
        dodd = jnp.dot(de[...], heven, preferred_element_type=f32)
        deven = jnp.dot(do[...], hodd, preferred_element_type=f32)
        he32 = hes[pl.ds(i0, OWN), :].astype(f32)
        ho32 = hos[pl.ds(i0, OWN), :].astype(f32)

        def place(t, lines):
            back = jnp.dot(flip_own, lines, preferred_element_type=f32)
            res = jnp.where(mirrored, back, lines.astype(f32))
            tx[r, :, t] = res.reshape(NZ, NB, NL).astype(bf16)

        place(0, (he32 + sign * ho32).astype(bf16))
        place(1, (deven + sign * dodd).astype(bf16))

    def energy_on():
        @pl.when(zh == 0)
        def _():
            pl.semaphore_wait(entered.at[NZ], 1)
            ecopy(e3, zh, es3.at[0], er3.at[zh], across).start()

        ecopy(e3, 1 - zh, es3.at[0], er3.at[1 - zh], across).wait_recv()
        e4[z] = jnp.sum(e3[...], axis=0)

        def send_e4(d, carry):
            ecopy(e4, z, es4.at[d], er4.at[z], at_z((z + d) % NZ)).start()
            return carry

        lax.fori_loop(1, NZ, send_e4, 0)

    def round_of(r):
        c, h = block(r, z)
        pltpu.make_async_copy(v_scr.at[c, h], rx.at[r, x * NZ + z], zr.at[r, z]).start()
        for g in range(NZ // NG):
            lax.fori_loop(0, NG, lambda q, cc, g=g: (zwait(r, group(g) + q), cc)[1], 0)
            for d in range(1, NX):
                xcopy(r, g, d).start()
        if r == 0:
            for w in wcopies:
                w.wait()
        for g in range(NZ // NG):
            for d in range(1, NX):
                xwait(r, g, d)
        compute(r)

        def send_back(i, carry):
            k = NZ - 1 - i

            @pl.when(z >= k)
            def _():
                bcopy(r, z - k).start()

            @pl.when(z + k < NZ)
            def _():
                bcopy(r, z + k).start()
            return carry

        lax.fori_loop(0, NZ - 1, send_back, 0)
        pltpu.make_async_copy(tx.at[r, z], rxo.at[h, c], br.at[h, c]).start()

    @pl.when(owner)
    def _():
        round_of(0)
        energy_on()
        round_of(1)

    @pl.when(extra)
    def _():
        round_of(NR)

    @pl.when(jnp.logical_not(owner))
    def _():
        for w in wcopies:
            w.wait()
        energy_on()

    kz = kz_ref[...].astype(f32) / KZ
    kz_sq = kz * kz

    def wait_e4(d, carry):
        p = (z + d) % NZ
        ecopy(e4, p, es4.at[d], er4.at[p], across).wait_recv()
        return carry

    lax.fori_loop(1, NZ, wait_e4, 0)
    energy = jnp.sum(jnp.sum(e4[...], axis=0), axis=1, keepdims=True)
    scale = jnp.float32(2.0 * KX * NY * KZ) / energy
    factors = []
    for k in range(KX):
        kx = kx_ref[k].astype(f32) / XMODES
        factors.append(scale * (1.0 / (1.0 + 2.0 * (kx * kx + kz_sq))))

    def bwait(r, q):
        pltpu.make_async_remote_copy(
            src_ref=tx.at[r, q], dst_ref=rxo.at[r, q],
            send_sem=bs.at[r, 0], recv_sem=br.at[r, q],
            device_id=across, device_id_type=MESH,
        ).wait_recv()

    for r in range(NR):
        h = r
        lax.fori_loop(0, NZ, lambda q, carry: (bwait(r, q), carry)[1], 0)
        for q in range(NZ):
            c = q
            f = factors[c % KX][:, h * NL:(h + 1) * NL]
            for t, out in enumerate((outu_ref, outd_ref)):
                out[c, :, h * NL:(h + 1) * NL] = (f * rxo[r, q, t].astype(f32)).astype(bf16)

    for r in range(NR + 1):
        for_owners(r, lambda p: zcopy(r, p).wait_send(), True)
        for_owners(r, lambda p: zcopy(r, p).wait_send(), False)

    def drain_round(r):
        lax.fori_loop(1, NZ, lambda d, cc: (bcopy(r, (z + d) % NZ).wait_send(), cc)[1], 0)
        for d in range(1, NX):
            for g in range(NZ // NG):
                xcopy(r, g, d).wait_send()

    @pl.when(owner)
    def _():
        for r in range(NR):
            drain_round(r)

    @pl.when(extra)
    def _():
        drain_round(NR)

    for d in range(1, NX):
        ecopy(e2, x, es2.at[d], er2.at[x], at_x(d)).wait_send()
    for d in range(1, 8):
        ecopy(e1, yc, es1.at[d], er1.at[yc], at_yc(d)).wait_send()

    ecopy(e3, zh, es3.at[0], er3.at[zh], across).wait_send()

    def drain_e4(d, carry):
        ecopy(e4, z, es4.at[d], er4.at[z], at_z((z + d) % NZ)).wait_send()
        return carry

    lax.fori_loop(1, NZ, drain_e4, 0)


def settle(u_ref, d_ref, outu_ref, outd_ref, sem):
    copies = [
        pltpu.make_async_copy(u_ref, outu_ref, sem.at[0]),
        pltpu.make_async_copy(d_ref, outd_ref, sem.at[1]),
    ]
    for c in copies:
        c.start()
    for c in copies:
        c.wait()


def local(velocity, kx_index, kz_index, helm_even, helm_odd, deriv_even, deriv_odd):
    v = velocity.reshape(NZ, NB, NC * NL)
    vm = pl.BlockSpec(memory_space=pltpu.VMEM)
    hbm = pl.BlockSpec(memory_space=pl.ANY)
    shape = jax.ShapeDtypeStruct((NZ, NB, NC * NL), bf16)
    dma = pltpu.SemaphoreType.DMA
    outu, outd = pl.pallas_call(
        kernel,
        out_shape=(pltpu.VMEM((NZ, NB, NC * NL), bf16),) * 2,
        in_specs=[hbm, pl.BlockSpec(memory_space=pltpu.SMEM), vm, hbm, hbm, hbm, hbm],
        out_specs=(vm, vm),
        scratch_shapes=[
            pltpu.VMEM((NZ, NC, NB, NL), bf16),
            pltpu.VMEM((NR + 1, NX * NZ, NB, NL), bf16),
            pltpu.VMEM((NR + 1, NZ, 2, NB, NL), bf16),
            pltpu.VMEM((NR, NZ, 2, NB, NL), bf16),
            pltpu.VMEM((HALF, HALF), bf16),
            pltpu.VMEM((HALF, HALF), bf16),
            pltpu.VMEM((OWN, HALF), bf16),
            pltpu.VMEM((OWN, HALF), bf16),
            pltpu.VMEM((HALF, NL), bf16),
            pltpu.VMEM((HALF, NL), bf16),
            pltpu.VMEM((8, 1, NL), f32),
            pltpu.VMEM((NX, 1, NL), f32),
            pltpu.VMEM((2, 1, NL), f32),
            pltpu.VMEM((NZ, 1, NL), f32),
            dma((NC,)), dma((4,)), pltpu.SemaphoreType.REGULAR((NZ + 1,)),
            dma((NR + 1, NZ)), dma((NR + 1, NZ)),
            dma((NR + 1, NZ // NG, NX)), dma((NR + 1, NZ // NG, NX)),
            dma((NR + 1, NZ)), dma((NR, NZ)),
            dma((8,)), dma((8,)), dma((NX,)), dma((NX,)),
            dma((1,)), dma((2,)), dma((NZ,)), dma((NZ,)),
        ],
        compiler_params=pltpu.CompilerParams(collective_id=0, has_side_effects=True),
    )(v, kx_index, kz_index.reshape(1, NC * NL), helm_even, helm_odd, deriv_even, deriv_odd)
    outu, outd = pl.pallas_call(
        settle, out_shape=(shape, shape), in_specs=[hbm, hbm], out_specs=(hbm, hbm),
        scratch_shapes=[dma((2,))], compiler_params=pltpu.CompilerParams(vmem_limit_bytes=2 ** 20),
    )(outu, outd)
    full = (2, KX, NB, NC * NL)
    return outu.reshape(full), outd.reshape(full)


def solution(mesh):
    in_specs = (P(None, None, "wall", "span"), P(), P("span"), P(), P(), P(), P())
    out_specs = (P(None, None, "wall", "span"), P(None, None, "wall", "span"))
    return jax.shard_map(local, mesh=mesh, in_specs=in_specs, out_specs=out_specs, check_vma=False)
```
